32 devices in a mesh: group: 2 (over x), mem: 16 (over z, y, core).
Axes of the slice: x: 2, y: 2, z: 4, core: 2. Of those that a mesh axis runs over, the one named last changes fastest.
Arguments:
- perturbations: bfloat16 [32, 256, 4, 1, 256], P(('group', 'mem')), parts along dimension 0, may hold values from -6 to 6
- gradient: bfloat16 [512, 4, 1, 256], P(('group', 'mem')), parts along dimension 0, may hold values from -6 to 6
Outputs:
- increment: bfloat16 [512, 4, 1, 256], P(('group', 'mem')), parts along dimension 0
The draws below stay inside these ranges and needn't reach their ends.
There are 2 independent parts, one for each index of `group`. The reference program is written for one: setup_inputs(seed, part) draws one part's arguments, and reference() takes and returns one part's arrays. A program takes and returns all parts, laid end to end along the dimension named above; each array names one. Nothing has to cross between parts.
All inputs are finite; a program needn't handle non-finite values.
Results may differ from the reference program's by a relative error of at most 0.0085.
Values may be sent and summed in bfloat16 or wider, within the bound.
No kernel may reach another device: no remote copies, remote signals or barrier semaphores. Data moves between devices by JAX's collectives and lax.ppermute only.
A program may use at most 64 MiB of HBM per device.

```python
import jax
import jax.numpy as jnp
from jax import lax

NY = 256
NX = 256
NVAR = 4
LEV = 1
REACH = 8
MEMBERS = 16


def raised(array, key, source, target, shards_of, factor):
    def block_of(axis_at):
        return (jnp.arange(array.shape[axis_at]) // (array.shape[axis_at] // shards_of)).reshape((-1,) + (1,) * (array.ndim - 1 - axis_at))

    near = jax.random.permutation(key, shards_of)[block_of(target)]
    other_side = (block_of(target) + shards_of // 2) % shards_of
    return jnp.where((block_of(source) == near) | (block_of(source) == other_side), factor * array, array)


def levels(rng, extent, shards, smallest, high):
    gain = 1.0
    for position, shards_of in shards:
        steps = jax.random.uniform(jax.random.fold_in(jax.random.fold_in(rng, 6), position), (shards_of,), jnp.float32, smallest / len(shards), high / len(shards))
        gain = gain * jnp.repeat(jnp.exp(steps), extent[position] // shards_of).reshape((-1,) + (1,) * (len(extent) - 1 - position))
    return gain


def gaussian(stream_key, shape, spread, most, cuts=(), kind=jnp.bfloat16):
    gain = levels(stream_key, shape, cuts, -0.22, 0.18) if cuts else 1.0
    values = jax.random.normal(stream_key, shape, jnp.float32) * spread * gain
    return jnp.minimum(jnp.maximum(values, -most), most).astype(kind)


def bell_draw_with(key, shape, scale, most, split, heavy, kind=jnp.bfloat16):
    result = scale * jax.random.normal(key, shape, jnp.float32)
    if split:
        result = result * levels(key, shape, split, -0.22, 0.18)
    return jnp.clip(raised(result, jax.random.fold_in(key, 3), *heavy), -most, most).astype(kind)


def setup_inputs(seed: int = 0, part: int = 0) -> dict:
    key_list = jax.random.split(jax.random.key(seed), 3)
    own_keys = jax.random.split(jax.random.fold_in(key_list[2], part), 3)
    return {
        "perturbations": bell_draw_with(own_keys[0], (MEMBERS, NY, NVAR, LEV, NX), 1.0, 6.0, ((0, 16),), (0, 1, 16, 2.0)),
        "gradient": gaussian(own_keys[1], (NY, NVAR, LEV, NX), 1.0, 6.0, ((0, 16),)),
    }


def make_band(order):
    rows = jnp.arange(order, dtype=jnp.int32)
    offset = (rows[:, None] - rows[None, :]).astype(jnp.float32)
    weights = jnp.exp(-(offset * offset) / (4.0 * REACH))
    inside = jnp.abs(offset) <= REACH
    return jnp.where(inside, weights, jnp.float32(0.0)).astype(jnp.bfloat16)


def reference(perturbations, gradient):
    band_x = make_band(NX)
    band_y = make_band(NY)
    grad_wide = gradient.astype(jnp.float32)

    def one_member(total, member):
        mixed = jnp.sum(member.astype(jnp.float32) * grad_wide, axis=1).astype(jnp.bfloat16)
        along_x = jnp.dot(mixed.reshape(NY * LEV, NX), band_x, preferred_element_type=jnp.float32).astype(jnp.bfloat16)
        filtered = jnp.dot(band_y, along_x.reshape(NY, LEV * NX), preferred_element_type=jnp.float32).astype(jnp.bfloat16)
        filtered = filtered.reshape(NY, 1, LEV, NX).astype(jnp.float32)
        return total + member.astype(jnp.float32) * filtered, None

    start = jnp.zeros((NY, NVAR, LEV, NX), jnp.float32)
    total, unused = lax.scan(one_member, start, perturbations)
    return (total * (1.0 / (MEMBERS - 1))).astype(jnp.bfloat16)
```

```python
import functools

import jax
import jax.numpy as jnp
from jax import lax
from jax.experimental import pallas as pl
from jax.experimental.pallas import tpu as pltpu
from jax.sharding import PartitionSpec as P

REACH = 8
GRANT = 16 << 20


def make_band(order):
    rows = jnp.arange(order, dtype=jnp.int32)
    offset = (rows[:, None] - rows[None, :]).astype(jnp.float32)
    weights = jnp.exp(-(offset * offset) / (4.0 * REACH))
    inside = jnp.abs(offset) <= REACH
    return jnp.where(inside, weights, jnp.float32(0.0)).astype(jnp.bfloat16)


def by_rows(perturbations, gradient):
    local_rows, nvars, levels, columns = gradient.shape
    count_here = perturbations.shape[0]
    grid_rows = perturbations.shape[1]
    members = count_here * lax.axis_size("mem")
    band_x = make_band(columns)
    band_y = make_band(grid_rows)
    row_block = lax.all_to_all(perturbations, "mem", split_axis=1, concat_axis=0, tiled=True)
    mixed = jnp.sum(
        row_block.astype(jnp.float32) * gradient.astype(jnp.float32)[None], axis=2
    ).astype(jnp.bfloat16)
    along_x = jnp.dot(
        mixed.reshape(members * local_rows * levels, columns),
        band_x,
        preferred_element_type=jnp.float32,
    )
    along_x = along_x.astype(jnp.bfloat16).reshape(members, local_rows, levels, columns)
    whole_field = lax.all_to_all(along_x, "mem", split_axis=0, concat_axis=1, tiled=True)
    whole_field = whole_field.reshape(count_here, grid_rows, levels * columns)
    filtered = jnp.stack(
        [jnp.dot(band_y, field, preferred_element_type=jnp.float32) for field in whole_field]
    )
    filtered = filtered.astype(jnp.bfloat16).reshape(count_here, grid_rows, levels, columns)
    row_field = lax.all_to_all(filtered, "mem", split_axis=1, concat_axis=0, tiled=True)
    total = jnp.sum(
        row_block.astype(jnp.float32) * row_field.astype(jnp.float32)[:, :, None], axis=0
    )
    return (total * (1.0 / (members - 1))).astype(jnp.bfloat16)


HALF, PAIR, SIDE, CORE = 8, 4, 2, 1
PEERS = (PAIR + SIDE, SIDE, PAIR)


def swap(array, bits):
    return lax.ppermute(array, "mem", [(i, i ^ bits) for i in range(16)])


def window_kernel(strip, me_ref, members_ref, *refs):
    outs, sem = refs[:-1], refs[-1]
    me = me_ref[0]
    rows = members_ref.shape[0]
    copies = []
    for bits, out in zip(PEERS + (0,), outs):
        for far in range(2):
            chip = ((me ^ bits) ^ (HALF * far)) // 2
            base = chip * strip
            for at, length in ((0, REACH), (REACH, strip), (REACH + strip, REACH)):
                start = jnp.clip(base + at - REACH, 0, rows - length)
                copies.append(
                    pltpu.make_async_copy(
                        members_ref.at[pl.ds(start, length)],
                        out.at[far, pl.ds(at, length)],
                        sem.at[len(copies)],
                    )
                )
    for copy in copies:
        copy.start()
    for copy in copies:
        copy.wait()


def windows(me, members, strip):
    rows, nvars, columns = members.shape
    shape = (2, strip + 2 * REACH, nvars, columns)
    return pl.pallas_call(
        functools.partial(window_kernel, strip),
        out_shape=[jax.ShapeDtypeStruct(shape, members.dtype)] * 4,
        in_specs=[pl.BlockSpec(memory_space=pltpu.SMEM), pl.BlockSpec(memory_space=pl.ANY)],
        out_specs=[pl.BlockSpec(memory_space=pltpu.VMEM)] * 4,
        scratch_shapes=[pltpu.SemaphoreType.DMA((24,))],
        compiler_params=pltpu.CompilerParams(vmem_limit_bytes=GRANT),
        name="windows",
    )(me, members)


def strip_kernel(strip, me_ref, a_ref, b_ref, c_ref, d_ref, here_ref, there_ref, mate_ref, band_x_ref, band_s_ref,
                 keep_ref, mate_out_ref, far_ref, far_mate_ref, grad_ref, mixed_ref, total_ref):
    core = me_ref[0] % 2
    part = here_ref.shape[0]
    own, other = pl.ds(core * part, part), pl.ds((1 - core) * part, part)
    grad_ref[0, own] = here_ref[...]
    grad_ref[1, own] = there_ref[...]
    grad_ref[0, other] = mate_ref[0]
    grad_ref[1, other] = mate_ref[1]
    span = strip + 2 * REACH
    members = (a_ref, b_ref, c_ref, d_ref)
    for far in range(2):
        grad = grad_ref[far].astype(jnp.float32)
        for k, ref in enumerate(members):
            mixed = jnp.sum(ref[far].astype(jnp.float32) * grad, axis=1)
            mixed_ref[pl.ds(k * span, span)] = mixed.astype(jnp.bfloat16)
        along = jnp.dot(mixed_ref[...], band_x_ref[...], preferred_element_type=jnp.float32).astype(jnp.bfloat16)
        total = None
        for k, ref in enumerate(members):
            field = jnp.dot(band_s_ref[...], along[k * span : (k + 1) * span], preferred_element_type=jnp.float32)
            field = field.astype(jnp.bfloat16).astype(jnp.float32)
            term = ref[far, REACH : REACH + strip].astype(jnp.float32) * field[:, None, :]
            total = term if total is None else total + term
        total_ref[far] = total
    half = strip // 2
    own, other = pl.ds(core * half, half), pl.ds((1 - core) * half, half)
    keep_ref[...] = total_ref[0, own]
    mate_out_ref[...] = total_ref[0, other].astype(jnp.bfloat16)
    far_ref[...] = total_ref[1, own].astype(jnp.bfloat16)
    far_mate_ref[...] = total_ref[1, other].astype(jnp.bfloat16)


def strips(me, members, here, there, mate, band_x, band_s, strip):
    _, span, nvars, columns = members[0].shape
    piece = (strip // 2, nvars, columns)
    vmem = pl.BlockSpec(memory_space=pltpu.VMEM)
    return pl.pallas_call(
        functools.partial(strip_kernel, strip),
        out_shape=[jax.ShapeDtypeStruct(piece, jnp.float32)] + [jax.ShapeDtypeStruct(piece, jnp.bfloat16)] * 3,
        in_specs=[pl.BlockSpec(memory_space=pltpu.SMEM)] + [vmem] * 9,
        out_specs=[vmem] * 4,
        scratch_shapes=[
            pltpu.VMEM((2, span, nvars, columns), jnp.bfloat16),
            pltpu.VMEM((4 * span, columns), jnp.bfloat16),
            pltpu.VMEM((2, strip, nvars, columns), jnp.float32),
        ],
        compiler_params=pltpu.CompilerParams(vmem_limit_bytes=GRANT),
        name="strips",
    )(me, *members, here, there, mate, band_x, band_s)


def by_halves(perturbations, gradient):
    local_rows, nvars, levels, columns = gradient.shape
    members = lax.axis_size("mem")
    strip = 2 * local_rows
    at = lax.axis_index("mem")
    me = at.reshape(1).astype(jnp.int32)
    first = at % 2 == 0
    grad = gradient.reshape(local_rows, nvars, columns)
    field = perturbations.reshape(-1, nvars, columns)

    edge = jnp.where(first, grad[:REACH], grad[-REACH:])
    across = [(i, i + 1) for i in range(1, 15, 2)] + [(i + 1, i) for i in range(1, 15, 2)]
    edge = lax.ppermute(edge, "mem", across)
    to_pair_side, to_side, to_pair, mine = windows(me, field, strip)
    here = jnp.where(first, jnp.concatenate([edge, grad]), jnp.concatenate([grad, edge]))
    got = [swap(block, bits) for block, bits in zip((to_pair_side, to_side, to_pair), PEERS)]
    there = swap(here, HALF)
    mate = swap(jnp.stack([here, there]), CORE)

    band_x = make_band(columns)
    band_s = make_band(strip + 2 * REACH)[REACH : REACH + strip]
    keep, to_mate, to_far, to_far_mate = strips(me, [mine] + got, here, there, mate, band_x, band_s, strip)
    total = (
        keep
        + swap(to_mate, CORE).astype(jnp.float32)
        + swap(to_far, HALF).astype(jnp.float32)
        + swap(to_far_mate, HALF + CORE).astype(jnp.float32)
    )
    return (total * (1.0 / (members - 1))).astype(jnp.bfloat16).reshape(gradient.shape)


def solution(mesh):
    def per_device(perturbations, gradient):
        count_here, grid_rows, nvars, levels, columns = perturbations.shape
        local_rows = gradient.shape[0]
        fits = count_here == 1 and levels == 1 and local_rows >= REACH and local_rows % 8 == 0
        if mesh.shape["mem"] == 16 and fits and grid_rows == 16 * local_rows:
            return by_halves(perturbations, gradient)
        return by_rows(perturbations, gradient)

    in_specs = (P(("group", "mem"), None, None, None, None), P(("group", "mem"), None, None, None))
    out_specs = P(("group", "mem"), None, None, None)
    return jax.shard_map(
        per_device, mesh=mesh, in_specs=in_specs, out_specs=out_specs, check_vma=False
    )
```

```python
import functools

import jax
import jax.numpy as jnp
from jax import lax
from jax.experimental import pallas as pl
from jax.experimental.pallas import tpu as pltpu
from jax.sharding import PartitionSpec as P


REACH = 8
GRANT = 16 << 20
FIRST_GRANT = 16 << 20


def make_band(order):
    rows = jnp.arange(order, dtype=jnp.int32)
    offset = (rows[:, None] - rows[None, :]).astype(jnp.float32)
    weights = jnp.exp(-(offset * offset) / (4.0 * REACH))
    inside = jnp.abs(offset) <= REACH
    return jnp.where(inside, weights, jnp.float32(0.0)).astype(jnp.bfloat16)


def by_rows(perturbations, gradient):
    local_rows, _, levels, columns = gradient.shape
    count_here = perturbations.shape[0]
    grid_rows = perturbations.shape[1]
    members = count_here * lax.axis_size("mem")
    band_x = make_band(columns)
    band_y = make_band(grid_rows)
    row_block = lax.all_to_all(perturbations, "mem", split_axis=1, concat_axis=0, tiled=True)
    mixed = jnp.sum(
        row_block.astype(jnp.float32) * gradient.astype(jnp.float32)[None], axis=2
    ).astype(jnp.bfloat16)
    along_x = jnp.dot(
        mixed.reshape(members * local_rows * levels, columns),
        band_x,
        preferred_element_type=jnp.float32,
    )
    along_x = along_x.astype(jnp.bfloat16).reshape(members, local_rows, levels, columns)
    whole_field = lax.all_to_all(along_x, "mem", split_axis=0, concat_axis=1, tiled=True)
    whole_field = whole_field.reshape(count_here, grid_rows, levels * columns)
    filtered = jnp.stack(
        [jnp.dot(band_y, field, preferred_element_type=jnp.float32) for field in whole_field]
    )
    filtered = filtered.astype(jnp.bfloat16).reshape(count_here, grid_rows, levels, columns)
    row_field = lax.all_to_all(filtered, "mem", split_axis=1, concat_axis=0, tiled=True)
    total = jnp.sum(
        row_block.astype(jnp.float32) * row_field.astype(jnp.float32)[:, :, None], axis=0
    )
    return (total * (1.0 / (members - 1))).astype(jnp.bfloat16)


HALF, PAIR, SIDE, CORE = 8, 4, 2, 1
PEERS = (PAIR + SIDE, SIDE, PAIR)


def swap(array, bits):
    return lax.ppermute(array, "mem", [(i, i ^ bits) for i in range(16)])


def edges(array):
    pairs = []
    for i in range(16):
        half, place, core = i // 8, i // 2 % 4, i % 2
        place = (place + (1 if core else 3)) % 4
        pairs.append((i, half * 8 + place * 2 + core))
    return lax.ppermute(array, "mem", pairs)


def first_row(strip, chip, rows):
    start = jnp.clip(chip * strip - REACH, 0, rows - strip - 2 * REACH)
    return start, chip * strip - start


def window_kernel(strip, wanted, me_ref, member_ref, *refs):
    outs, sem = refs[:-1], refs[-1]
    me = me_ref[0]
    rows = member_ref.shape[0]
    copies = []
    for bits, out in zip(wanted, outs):
        start, _ = first_row(strip, (me ^ bits) // 2, rows)
        copies.append(pltpu.make_async_copy(member_ref.at[pl.ds(start, strip + 2 * REACH)], out, sem.at[len(copies)]))
    for copy in copies:
        copy.start()
    for copy in copies:
        copy.wait()


def windows(me, member, strip, wanted, grant):
    _, nvars, columns = member.shape
    shape = (strip + 2 * REACH, nvars, columns)
    count = len(wanted)
    return pl.pallas_call(
        functools.partial(window_kernel, strip, wanted),
        out_shape=[jax.ShapeDtypeStruct(shape, member.dtype)] * count,
        in_specs=[pl.BlockSpec(memory_space=pltpu.SMEM), pl.BlockSpec(memory_space=pltpu.HBM)],
        out_specs=[pl.BlockSpec(memory_space=pltpu.VMEM)] * count,
        scratch_shapes=[pltpu.SemaphoreType.DMA((count,))],
        compiler_params=pltpu.CompilerParams(vmem_limit_bytes=grant),
    )(me, member)


def strip_kernel(rows, far, me_ref, a_ref, b_ref, c_ref, d_ref, block_ref, mate_ref, edge_ref, edge_mate_ref, band_ref,
                 own_ref, other_ref, grad_ref, mixed_ref, total_ref):
    me = me_ref[0]
    core, place = me % 2, me // 2 % 4
    part, reach = block_ref.shape[0], edge_ref.shape[1]
    strip = 2 * part
    chips = rows // strip
    chip = (me ^ (HALF * far)) // 2
    _, at = first_row(strip, chip, rows)
    span = strip + 2 * reach

    grad_ref[...] = jnp.zeros_like(grad_ref)
    grad_ref[pl.ds(at + core * part, part)] = block_ref[...]
    grad_ref[pl.ds(at + (1 - core) * part, part)] = mate_ref[...]
    before = jnp.where(place == 0, 1 - far, far)
    after = jnp.where(place == 3, 1 - far, far)

    @pl.when(jnp.logical_and(chip > 0, core == 0))
    def _():
        grad_ref[pl.ds(at - reach, reach)] = edge_mate_ref[before]

    @pl.when(jnp.logical_and(chip > 0, core == 1))
    def _():
        grad_ref[pl.ds(at - reach, reach)] = edge_ref[before]

    @pl.when(jnp.logical_and(chip < chips - 1, core == 0))
    def _():
        grad_ref[pl.ds(at + strip, reach)] = edge_ref[after]

    @pl.when(jnp.logical_and(chip < chips - 1, core == 1))
    def _():
        grad_ref[pl.ds(at + strip, reach)] = edge_mate_ref[after]

    grad = grad_ref[...].astype(jnp.float32)
    members = (a_ref, b_ref, c_ref, d_ref)
    for k, ref in enumerate(members):
        mixed = jnp.sum(ref[...].astype(jnp.float32) * grad, axis=1)
        mixed_ref[pl.ds(k * span, span)] = mixed.astype(jnp.bfloat16)
    along = jnp.dot(mixed_ref[...], band_ref[...], preferred_element_type=jnp.float32).astype(jnp.bfloat16)
    offset = lax.broadcasted_iota(jnp.int32, (strip, span), 0) + at - lax.broadcasted_iota(jnp.int32, (strip, span), 1)
    wide = offset.astype(jnp.float32)
    band = jnp.exp(-(wide * wide) / (4.0 * REACH))
    band = jnp.where(jnp.abs(wide) <= REACH, band, 0.0).astype(jnp.bfloat16)
    total = None
    for k, ref in enumerate(members):
        field = jnp.dot(band, along[k * span : (k + 1) * span], preferred_element_type=jnp.float32)
        field = field.astype(jnp.bfloat16).astype(jnp.float32)
        term = ref[pl.ds(at, strip)].astype(jnp.float32) * field[:, None, :]
        total = term if total is None else total + term
    total_ref[...] = total
    own_ref[...] = total_ref[pl.ds(core * part, part)].astype(own_ref.dtype)
    other_ref[...] = total_ref[pl.ds((1 - core) * part, part)].astype(other_ref.dtype)


def one_strip(me, members, block, mate, edge, edge_mate, band, rows, far):
    span, nvars, columns = members[0].shape
    part = block.shape[0]
    piece = (part, nvars, columns)
    vmem = pl.BlockSpec(memory_space=pltpu.VMEM)
    return pl.pallas_call(
        functools.partial(strip_kernel, rows, far),
        out_shape=[
            jax.ShapeDtypeStruct(piece, jnp.bfloat16 if far else jnp.float32),
            jax.ShapeDtypeStruct(piece, jnp.bfloat16),
        ],
        in_specs=[pl.BlockSpec(memory_space=pltpu.SMEM)] + [vmem] * 9,
        out_specs=[vmem] * 2,
        scratch_shapes=[
            pltpu.VMEM((span, nvars, columns), jnp.bfloat16),
            pltpu.VMEM((4 * span, columns), jnp.bfloat16),
            pltpu.VMEM((2 * part, nvars, columns), jnp.float32),
        ],
        compiler_params=pltpu.CompilerParams(vmem_limit_bytes=GRANT),
        name="far" if far else "near",
    )(me, *members, block, mate, edge, edge_mate, band)


def by_halves(perturbations, gradient):
    local_rows, nvars, _, columns = gradient.shape
    grid_rows = perturbations.shape[1]
    strip = 2 * local_rows
    members = lax.axis_size("mem")
    at = lax.axis_index("mem")
    me = at.reshape(1).astype(jnp.int32)
    here = gradient.reshape(local_rows, nvars, columns)
    member = perturbations.reshape(-1, nvars, columns)

    far_out = windows(me, member, strip, [p ^ HALF for p in PEERS], FIRST_GRANT)
    far_in = [swap(block, p) for block, p in zip(far_out, PEERS)]
    there = swap(here, HALF)
    *near_out, near_mine, far_mine = windows(me, member, strip, list(PEERS) + [0, HALF], GRANT)
    near_in = [swap(block, p) for block, p in zip(near_out, PEERS)]
    here_mate = swap(here, CORE)
    both = jnp.stack([here, there])
    both = jnp.where(at & 1 == 0, both[:, :REACH], both[:, -REACH:])
    edge = edges(both)
    there_mate = swap(there, CORE)
    edge_mate = swap(edge, CORE)

    band = make_band(columns)
    args = (edge, edge_mate, band, grid_rows)
    far_own, far_other = one_strip(me, [far_mine] + far_in, there, there_mate, *args, 1)
    far_own, far_other = swap(far_own, HALF), swap(far_other, HALF + CORE)
    near_own, near_other = one_strip(me, [near_mine] + near_in, here, here_mate, *args, 0)
    near_other = swap(near_other, CORE)
    total = near_own + near_other.astype(jnp.float32) + far_own.astype(jnp.float32) + far_other.astype(jnp.float32)
    return (total * (1.0 / (members - 1))).astype(jnp.bfloat16).reshape(gradient.shape)


def solution(mesh):
    in_specs = (P(("group", "mem"), None, None, None, None), P(("group", "mem"), None, None, None))
    out_specs = P(("group", "mem"), None, None, None)
    halves = mesh.shape["mem"] == 16

    def per_device(perturbations, gradient):
        count_here, grid_rows, _, levels, _ = perturbations.shape
        local_rows = gradient.shape[0]
        if not halves:
            return by_rows(perturbations, gradient)
        assert count_here == 1 and levels == 1 and local_rows % 8 == 0 and grid_rows == 16 * local_rows
        return by_halves(perturbations, gradient)

    return jax.shard_map(
        per_device, mesh=mesh, in_specs=in_specs, out_specs=out_specs, check_vma=False
    )
```

```python
import functools

import jax
import jax.numpy as jnp
from jax import lax
from jax.experimental import pallas as pl
from jax.experimental.pallas import tpu as pltpu
from jax.sharding import PartitionSpec as P


REACH = 8
GRANT = 16 << 20


def make_band(order):
    rows = jnp.arange(order, dtype=jnp.int32)
    offset = (rows[:, None] - rows[None, :]).astype(jnp.float32)
    weights = jnp.exp(-(offset * offset) / (4.0 * REACH))
    inside = jnp.abs(offset) <= REACH
    return jnp.where(inside, weights, jnp.float32(0.0)).astype(jnp.bfloat16)


def by_rows(perturbations, gradient):
    local_rows, _, levels, columns = gradient.shape
    count_here = perturbations.shape[0]
    grid_rows = perturbations.shape[1]
    members = count_here * lax.axis_size("mem")
    band_x = make_band(columns)
    band_y = make_band(grid_rows)
    row_block = lax.all_to_all(perturbations, "mem", split_axis=1, concat_axis=0, tiled=True)
    mixed = jnp.sum(
        row_block.astype(jnp.float32) * gradient.astype(jnp.float32)[None], axis=2
    ).astype(jnp.bfloat16)
    along_x = jnp.dot(
        mixed.reshape(members * local_rows * levels, columns),
        band_x,
        preferred_element_type=jnp.float32,
    )
    along_x = along_x.astype(jnp.bfloat16).reshape(members, local_rows, levels, columns)
    whole_field = lax.all_to_all(along_x, "mem", split_axis=0, concat_axis=1, tiled=True)
    whole_field = whole_field.reshape(count_here, grid_rows, levels * columns)
    filtered = jnp.stack(
        [jnp.dot(band_y, field, preferred_element_type=jnp.float32) for field in whole_field]
    )
    filtered = filtered.astype(jnp.bfloat16).reshape(count_here, grid_rows, levels, columns)
    row_field = lax.all_to_all(filtered, "mem", split_axis=1, concat_axis=0, tiled=True)
    total = jnp.sum(
        row_block.astype(jnp.float32) * row_field.astype(jnp.float32)[:, :, None], axis=0
    )
    return (total * (1.0 / (members - 1))).astype(jnp.bfloat16)


HALF, PAIR, SIDE, CORE = 8, 4, 2, 1
PEERS = (PAIR + SIDE, SIDE, PAIR)
SPLIT = (6, 2, 4)
DIRECT = False
CHAIN = True


def swap(array, bits):
    return lax.ppermute(array, "mem", [(i, i ^ bits) for i in range(16)])


def edges(array, bits=0):
    pairs = []
    for i in range(16):
        chip = i // 2 + (1 if i % 2 else -1)
        if DIRECT and not 0 <= chip < 8:
            continue
        chip = chip if DIRECT else i // 8 * 4 + chip % 4
        pairs.append((i, (2 * chip + i % 2) ^ bits))
    return lax.ppermute(array, "mem", pairs)


def first_row(strip, chip, rows):
    start = jnp.clip(chip * strip - REACH, 0, rows - strip - 2 * REACH)
    return start, chip * strip - start


def window_kernel(strip, wanted, me_ref, member_ref, grad_ref, *refs):
    outs, sem = refs[:-1], refs[-1]
    me = me_ref[0]
    rows, part = member_ref.shape[0], grad_ref.shape[0]
    copies = []

    def add(source, out):
        copies.append(pltpu.make_async_copy(source, out, sem.at[len(copies)]))

    for bits, out in zip(wanted, outs):
        both = isinstance(bits, tuple)
        for k, bit in enumerate(bits if both else (bits,)):
            start, _ = first_row(strip, (me ^ bit) // 2, rows)
            add(member_ref.at[pl.ds(start, strip + 2 * REACH)], out.at[k] if both else out)
    add(grad_ref, outs[len(wanted)])
    if DIRECT:
        add(grad_ref.at[pl.ds((me % 2) * (part - REACH), REACH)], outs[len(wanted) + 1])
    for copy in copies:
        copy.start()
    for copy in copies:
        copy.wait()


def windows(me, member, grad, strip, wanted):
    _, nvars, columns = member.shape
    shape = (strip + 2 * REACH, nvars, columns)
    outs = [jax.ShapeDtypeStruct((2,) + shape if isinstance(bits, tuple) else shape, member.dtype) for bits in wanted]
    outs.append(jax.ShapeDtypeStruct(grad.shape, grad.dtype))
    if DIRECT:
        outs.append(jax.ShapeDtypeStruct((REACH,) + grad.shape[1:], grad.dtype))
    return pl.pallas_call(
        functools.partial(window_kernel, strip, wanted),
        out_shape=outs,
        in_specs=[pl.BlockSpec(memory_space=pltpu.SMEM)] + [pl.BlockSpec(memory_space=pltpu.HBM)] * 2,
        out_specs=[pl.BlockSpec(memory_space=pltpu.VMEM)] * len(outs),
        scratch_shapes=[pltpu.SemaphoreType.DMA((2 * len(outs),))],
        compiler_params=pltpu.CompilerParams(vmem_limit_bytes=GRANT),
    )(me, member, grad)


def strip_kernel(rows, far, me_ref, a_ref, b_ref, c_ref, d_ref, block_ref, edge_ref, mate_ref, band_ref,
                 own_ref, other_ref, grad_ref, mixed_ref, total_ref):
    me = me_ref[0]
    core, place = me % 2, me // 2 % 4
    part, reach = block_ref.shape[0], edge_ref.shape[1]
    strip = 2 * part
    chips = rows // strip
    chip = (me ^ (HALF * far)) // 2
    _, at = first_row(strip, chip, rows)
    span = strip + 2 * reach

    grad_ref[...] = jnp.zeros_like(grad_ref)
    grad_ref[pl.ds(at + core * part, part)] = block_ref[...]
    grad_ref[pl.ds(at + (1 - core) * part, part)] = mate_ref[pl.ds(far * part, part)]
    before = far if DIRECT else jnp.where(place == 0, 1 - far, far)
    after = far if DIRECT else jnp.where(place == 3, 1 - far, far)

    @pl.when(jnp.logical_and(chip > 0, core == 0))
    def _():
        grad_ref[pl.ds(at - reach, reach)] = mate_ref[pl.ds(2 * part + before * reach, reach)]

    @pl.when(jnp.logical_and(chip > 0, core == 1))
    def _():
        grad_ref[pl.ds(at - reach, reach)] = edge_ref[before]

    @pl.when(jnp.logical_and(chip < chips - 1, core == 0))
    def _():
        grad_ref[pl.ds(at + strip, reach)] = edge_ref[after]

    @pl.when(jnp.logical_and(chip < chips - 1, core == 1))
    def _():
        grad_ref[pl.ds(at + strip, reach)] = mate_ref[pl.ds(2 * part + after * reach, reach)]

    grad = grad_ref[...].astype(jnp.float32)
    members = [ref.at[far] if len(ref.shape) == 4 else ref for ref in (a_ref, b_ref, c_ref, d_ref)]
    for k, ref in enumerate(members):
        mixed = jnp.sum(ref[...].astype(jnp.float32) * grad, axis=1)
        mixed_ref[pl.ds(k * span, span)] = mixed.astype(jnp.bfloat16)
    along = jnp.dot(mixed_ref[...], band_ref[...], preferred_element_type=jnp.float32).astype(jnp.bfloat16)
    offset = lax.broadcasted_iota(jnp.int32, (strip, span), 0) + at - lax.broadcasted_iota(jnp.int32, (strip, span), 1)
    wide = offset.astype(jnp.float32)
    band = jnp.exp(-(wide * wide) / (4.0 * REACH))
    band = jnp.where(jnp.abs(wide) <= REACH, band, 0.0).astype(jnp.bfloat16)
    total = None
    for k, ref in enumerate(members):
        field = jnp.dot(band, along[k * span : (k + 1) * span], preferred_element_type=jnp.float32)
        field = field.astype(jnp.bfloat16).astype(jnp.float32)
        term = ref[pl.ds(at, strip)].astype(jnp.float32) * field[:, None, :]
        total = term if total is None else total + term
    total_ref[...] = total
    own_ref[...] = total_ref[pl.ds(core * part, part)].astype(own_ref.dtype)
    other_ref[...] = total_ref[pl.ds((1 - core) * part, part)].astype(other_ref.dtype)


def one_strip(me, members, block, edge, mate, band, rows, far):
    nvars, columns = block.shape[1:]
    part = block.shape[0]
    span = 2 * part + 2 * edge.shape[1]
    piece = (part, nvars, columns)
    vmem = pl.BlockSpec(memory_space=pltpu.VMEM)
    return pl.pallas_call(
        functools.partial(strip_kernel, rows, far),
        out_shape=[
            jax.ShapeDtypeStruct(piece, jnp.float32 if CHAIN or not far else jnp.bfloat16),
            jax.ShapeDtypeStruct(piece, jnp.bfloat16),
        ],
        in_specs=[pl.BlockSpec(memory_space=pltpu.SMEM)] + [vmem] * 8,
        out_specs=[vmem] * 2,
        scratch_shapes=[
            pltpu.VMEM((span, nvars, columns), jnp.bfloat16),
            pltpu.VMEM((4 * span, columns), jnp.bfloat16),
            pltpu.VMEM((2 * part, nvars, columns), jnp.float32),
        ],
        compiler_params=pltpu.CompilerParams(vmem_limit_bytes=GRANT),
        name="far" if far else "near",
    )(me, *members, block, edge, mate, band)


def by_halves(perturbations, gradient):
    local_rows, nvars, _, columns = gradient.shape
    grid_rows = perturbations.shape[1]
    strip = 2 * local_rows
    members = lax.axis_size("mem")
    at = lax.axis_index("mem")
    me = at.reshape(1).astype(jnp.int32)
    param = gradient.reshape(local_rows, nvars, columns)
    member = pltpu.with_memory_space_constraint(perturbations.reshape(-1, nvars, columns), pltpu.HBM)
    stays = pltpu.with_memory_space_constraint(param, pltpu.HBM)

    wanted = []
    for p in PEERS:
        wanted += [p ^ HALF, p] if p in SPLIT else [(p, p ^ HALF)]
    out = list(windows(me, member, stays, strip, wanted + [(0, HALF)]))
    mine, here = out[len(wanted)], out[len(wanted) + 1]
    edge_out = out[-1]
    far_in, near_in = [mine], [mine]
    for p in PEERS:
        if p in SPLIT:
            far_in.append(swap(out.pop(0), p))
            near_in.append(swap(out.pop(0), p))
        else:
            both = swap(out.pop(0), p)
            far_in.append(both)
            near_in.append(both)
    there = swap(here, HALF)
    if DIRECT:
        edge = jnp.stack([edges(edge_out), edges(edge_out, HALF)])
    else:
        both = jnp.stack([here, there])
        both = jnp.where(at & 1 == 0, both[:, :REACH], both[:, -REACH:])
        edge = edges(both)
    mate = swap(jnp.concatenate([here, there, edge[0], edge[1]]), CORE)

    band = make_band(columns)
    args = (edge, mate, band, grid_rows)
    far_own, far_other = one_strip(me, far_in, there, *args, 1)
    if CHAIN:
        far_sum = far_own + swap(far_other, CORE).astype(jnp.float32)
        far_sum = swap(far_sum.astype(jnp.bfloat16), HALF).astype(jnp.float32)
    else:
        far_own, far_other = swap(far_own, HALF), swap(far_other, HALF + CORE)
        far_sum = far_own.astype(jnp.float32) + far_other.astype(jnp.float32)
    near_own, near_other = one_strip(me, near_in, here, *args, 0)
    near_other = swap(near_other, CORE)
    total = near_own + near_other.astype(jnp.float32) + far_sum
    return (total * (1.0 / (members - 1))).astype(jnp.bfloat16).reshape(gradient.shape)


def solution(mesh):
    in_specs = (P(("group", "mem"), None, None, None, None), P(("group", "mem"), None, None, None))
    out_specs = P(("group", "mem"), None, None, None)
    halves = mesh.shape["mem"] == 16

    def per_device(perturbations, gradient):
        count_here, grid_rows, _, levels, _ = perturbations.shape
        local_rows = gradient.shape[0]
        if not halves:
            return by_rows(perturbations, gradient)
        assert count_here == 1 and levels == 1 and local_rows % 8 == 0 and grid_rows == 16 * local_rows
        return by_halves(perturbations, gradient)

    return jax.shard_map(
        per_device, mesh=mesh, in_specs=in_specs, out_specs=out_specs, check_vma=False
    )
```

```python
import functools

import jax
import jax.numpy as jnp
from jax import lax
from jax.experimental import pallas as pl
from jax.experimental.pallas import tpu as pltpu
from jax.sharding import PartitionSpec as P


REACH = 8
GRANT = 16 << 20


def make_band(order):
    rows = jnp.arange(order, dtype=jnp.int32)
    offset = (rows[:, None] - rows[None, :]).astype(jnp.float32)
    weights = jnp.exp(-(offset * offset) / (4.0 * REACH))
    inside = jnp.abs(offset) <= REACH
    return jnp.where(inside, weights, jnp.float32(0.0)).astype(jnp.bfloat16)


def by_rows(perturbations, gradient):
    local_rows, _, levels, columns = gradient.shape
    count_here = perturbations.shape[0]
    grid_rows = perturbations.shape[1]
    members = count_here * lax.axis_size("mem")
    band_x = make_band(columns)
    band_y = make_band(grid_rows)
    row_block = lax.all_to_all(perturbations, "mem", split_axis=1, concat_axis=0, tiled=True)
    mixed = jnp.sum(
        row_block.astype(jnp.float32) * gradient.astype(jnp.float32)[None], axis=2
    ).astype(jnp.bfloat16)
    along_x = jnp.dot(
        mixed.reshape(members * local_rows * levels, columns),
        band_x,
        preferred_element_type=jnp.float32,
    )
    along_x = along_x.astype(jnp.bfloat16).reshape(members, local_rows, levels, columns)
    whole_field = lax.all_to_all(along_x, "mem", split_axis=0, concat_axis=1, tiled=True)
    whole_field = whole_field.reshape(count_here, grid_rows, levels * columns)
    filtered = jnp.stack(
        [jnp.dot(band_y, field, preferred_element_type=jnp.float32) for field in whole_field]
    )
    filtered = filtered.astype(jnp.bfloat16).reshape(count_here, grid_rows, levels, columns)
    row_field = lax.all_to_all(filtered, "mem", split_axis=1, concat_axis=0, tiled=True)
    total = jnp.sum(
        row_block.astype(jnp.float32) * row_field.astype(jnp.float32)[:, :, None], axis=0
    )
    return (total * (1.0 / (members - 1))).astype(jnp.bfloat16)


HALF, PAIR, SIDE, CORE = 8, 4, 2, 1
PEERS = (PAIR + SIDE, SIDE, PAIR)
SPLIT = (6, 2, 4)
DIRECT = False
CHAIN = True


def swap(array, bits):
    return lax.ppermute(array, "mem", [(i, i ^ bits) for i in range(16)])


def edges(array, bits=0):
    pairs = []
    for i in range(16):
        chip = i // 2 + (1 if i % 2 else -1)
        if DIRECT and not 0 <= chip < 8:
            continue
        chip = chip if DIRECT else i // 8 * 4 + chip % 4
        pairs.append((i, (2 * chip + i % 2) ^ bits))
    return lax.ppermute(array, "mem", pairs)


def first_row(strip, chip, rows):
    start = jnp.clip(chip * strip - REACH, 0, rows - strip - 2 * REACH)
    return start, chip * strip - start


def window_kernel(strip, wanted, me_ref, member_ref, grad_ref, *refs):
    outs, sem = refs[:-1], refs[-1]
    me = me_ref[0]
    rows = member_ref.shape[0]
    copies = []

    def add(source, out):
        copies.append(pltpu.make_async_copy(source, out, sem.at[len(copies)]))

    for bits, out in zip(wanted, outs):
        both = isinstance(bits, tuple)
        for k, bit in enumerate(bits if both else (bits,)):
            start, _ = first_row(strip, (me ^ bit) // 2, rows)
            add(member_ref.at[pl.ds(start, strip + 2 * REACH)], out.at[k] if both else out)
    if len(outs) > len(wanted):
        add(grad_ref, outs[len(wanted)])
    for copy in copies:
        copy.start()
    for copy in copies:
        copy.wait()


def windows(me, member, grad, strip, wanted, keep=True):
    _, nvars, columns = member.shape
    shape = (strip + 2 * REACH, nvars, columns)
    outs = [jax.ShapeDtypeStruct((2,) + shape if isinstance(bits, tuple) else shape, member.dtype) for bits in wanted]
    if keep:
        outs.append(jax.ShapeDtypeStruct(grad.shape, grad.dtype))
    return pl.pallas_call(
        functools.partial(window_kernel, strip, wanted),
        out_shape=outs,
        in_specs=[pl.BlockSpec(memory_space=pltpu.SMEM)] + [pl.BlockSpec(memory_space=pltpu.HBM)] * 2,
        out_specs=[pl.BlockSpec(memory_space=pltpu.VMEM)] * len(outs),
        scratch_shapes=[pltpu.SemaphoreType.DMA((2 * len(outs),))],
        compiler_params=pltpu.CompilerParams(vmem_limit_bytes=GRANT),
    )(me, member, grad)


def strip_kernel(rows, far, me_ref, a_ref, b_ref, c_ref, d_ref, block_ref, edge_ref, mate_ref, band_ref,
                 own_ref, other_ref, grad_ref, mixed_ref, total_ref):
    me = me_ref[0]
    core, place = me % 2, me // 2 % 4
    part, reach = block_ref.shape[0], edge_ref.shape[1]
    strip = 2 * part
    chips = rows // strip
    chip = (me ^ (HALF * far)) // 2
    _, at = first_row(strip, chip, rows)
    span = strip + 2 * reach

    grad_ref[...] = jnp.zeros_like(grad_ref)
    grad_ref[pl.ds(at + core * part, part)] = block_ref[...]
    grad_ref[pl.ds(at + (1 - core) * part, part)] = mate_ref[pl.ds(far * part, part)]
    before = far if DIRECT else jnp.where(place == 0, 1 - far, far)
    after = far if DIRECT else jnp.where(place == 3, 1 - far, far)

    @pl.when(jnp.logical_and(chip > 0, core == 0))
    def _():
        grad_ref[pl.ds(at - reach, reach)] = mate_ref[pl.ds(2 * part + before * reach, reach)]

    @pl.when(jnp.logical_and(chip > 0, core == 1))
    def _():
        grad_ref[pl.ds(at - reach, reach)] = edge_ref[before]

    @pl.when(jnp.logical_and(chip < chips - 1, core == 0))
    def _():
        grad_ref[pl.ds(at + strip, reach)] = edge_ref[after]

    @pl.when(jnp.logical_and(chip < chips - 1, core == 1))
    def _():
        grad_ref[pl.ds(at + strip, reach)] = mate_ref[pl.ds(2 * part + after * reach, reach)]

    grad = grad_ref[...].astype(jnp.float32)
    members = [ref.at[far] if len(ref.shape) == 4 else ref for ref in (a_ref, b_ref, c_ref, d_ref)]
    nvars, columns = grad.shape[1:]
    grad = grad.reshape(span * nvars, columns)
    row = lax.broadcasted_iota(jnp.int32, (span, span * nvars), 1) // nvars
    pick = jnp.where(row == lax.broadcasted_iota(jnp.int32, row.shape, 0), 1.0, 0.0).astype(jnp.bfloat16)
    for k, ref in enumerate(members):
        terms = ref[...].reshape(span * nvars, columns).astype(jnp.float32) * grad
        high = terms.astype(jnp.bfloat16)
        low = (terms - high.astype(jnp.float32)).astype(jnp.bfloat16)
        mixed = jnp.dot(pick, high, preferred_element_type=jnp.float32)
        mixed = mixed + jnp.dot(pick, low, preferred_element_type=jnp.float32)
        mixed_ref[pl.ds(k * span, span)] = mixed.astype(jnp.bfloat16)
    along = jnp.dot(mixed_ref[...], band_ref[...], preferred_element_type=jnp.float32).astype(jnp.bfloat16)
    offset = lax.broadcasted_iota(jnp.int32, (strip, span), 0) + at - lax.broadcasted_iota(jnp.int32, (strip, span), 1)
    wide = offset.astype(jnp.float32)
    band = jnp.exp(-(wide * wide) / (4.0 * REACH))
    band = jnp.where(jnp.abs(wide) <= REACH, band, 0.0).astype(jnp.bfloat16)
    total = None
    for k, ref in enumerate(members):
        field = jnp.dot(band, along[k * span : (k + 1) * span], preferred_element_type=jnp.float32)
        field = field.astype(jnp.bfloat16).astype(jnp.float32)
        term = ref[pl.ds(at, strip)].astype(jnp.float32) * field[:, None, :]
        total = term if total is None else total + term
    total_ref[...] = total
    own_ref[...] = total_ref[pl.ds(core * part, part)].astype(own_ref.dtype)
    other_ref[...] = total_ref[pl.ds((1 - core) * part, part)].astype(other_ref.dtype)


def one_strip(me, members, block, edge, mate, band, rows, far):
    nvars, columns = block.shape[1:]
    part = block.shape[0]
    span = 2 * part + 2 * edge.shape[1]
    piece = (part, nvars, columns)
    vmem = pl.BlockSpec(memory_space=pltpu.VMEM)
    return pl.pallas_call(
        functools.partial(strip_kernel, rows, far),
        out_shape=[
            jax.ShapeDtypeStruct(piece, jnp.float32 if CHAIN or not far else jnp.bfloat16),
            jax.ShapeDtypeStruct(piece, jnp.bfloat16),
        ],
        in_specs=[pl.BlockSpec(memory_space=pltpu.SMEM)] + [vmem] * 8,
        out_specs=[vmem] * 2,
        scratch_shapes=[
            pltpu.VMEM((span, nvars, columns), jnp.bfloat16),
            pltpu.VMEM((4 * span, columns), jnp.bfloat16),
            pltpu.VMEM((2 * part, nvars, columns), jnp.float32),
        ],
        compiler_params=pltpu.CompilerParams(vmem_limit_bytes=GRANT),
        name="far" if far else "near",
    )(me, *members, block, edge, mate, band)


def by_halves(perturbations, gradient):
    local_rows, nvars, _, columns = gradient.shape
    grid_rows = perturbations.shape[1]
    strip = 2 * local_rows
    members = lax.axis_size("mem")
    at = lax.axis_index("mem")
    me = at.reshape(1).astype(jnp.int32)
    param = gradient.reshape(local_rows, nvars, columns)
    member = pltpu.with_memory_space_constraint(perturbations.reshape(-1, nvars, columns), pltpu.HBM)
    stays = pltpu.with_memory_space_constraint(param, pltpu.HBM)

    wanted = []
    for p in PEERS:
        wanted += [p ^ HALF, p] if p in SPLIT else [(p, p ^ HALF)]
    wanted.append((0, HALF))
    cut = 99
    out = list(windows(me, member, stays, strip, wanted[:cut]))
    here = out.pop()
    if cut < len(wanted):
        out += windows(me, member, stays, strip, wanted[cut:], False)
    mine = out[-1]
    far_in, near_in = [mine], [mine]
    for p in PEERS:
        if p in SPLIT:
            far_in.append(swap(out.pop(0), p))
            near_in.append(swap(out.pop(0), p))
        else:
            both = swap(out.pop(0), p)
            far_in.append(both)
            near_in.append(both)
    there = swap(param, HALF)
    if DIRECT:
        edge = jnp.stack([edges(edge_out), edges(edge_out, HALF)])
    else:
        both = jnp.stack([here, there])
        both = jnp.where(at & 1 == 0, both[:, :REACH], both[:, -REACH:])
        edge = edges(both)
    mate = swap(jnp.concatenate([here, there, edge[0], edge[1]]), CORE)

    band = make_band(columns)
    args = (edge, mate, band, grid_rows)
    far_own, far_other = one_strip(me, far_in, there, *args, 1)
    if CHAIN:
        far_sum = far_own + swap(far_other, CORE).astype(jnp.float32)
        far_sum = swap(far_sum.astype(jnp.bfloat16), HALF).astype(jnp.float32)
    else:
        far_own, far_other = swap(far_own, HALF), swap(far_other, HALF + CORE)
        far_sum = far_own.astype(jnp.float32) + far_other.astype(jnp.float32)
    near_own, near_other = one_strip(me, near_in, here, *args, 0)
    near_other = swap(near_other, CORE)
    total = near_own + near_other.astype(jnp.float32) + far_sum
    return (total * (1.0 / (members - 1))).astype(jnp.bfloat16).reshape(gradient.shape)


def solution(mesh):
    in_specs = (P(("group", "mem"), None, None, None, None), P(("group", "mem"), None, None, None))
    out_specs = P(("group", "mem"), None, None, None)
    halves = mesh.shape["mem"] == 16

    def per_device(perturbations, gradient):
        count_here, grid_rows, _, levels, _ = perturbations.shape
        local_rows = gradient.shape[0]
        if not halves:
            return by_rows(perturbations, gradient)
        assert count_here == 1 and levels == 1 and local_rows % 8 == 0 and grid_rows == 16 * local_rows
        return by_halves(perturbations, gradient)

    return jax.shard_map(
        per_device, mesh=mesh, in_specs=in_specs, out_specs=out_specs, check_vma=False
    )
```

```python
import functools

import jax
import jax.numpy as jnp
from jax import lax
from jax.experimental import pallas as pl
from jax.experimental.pallas import tpu as pltpu
from jax.sharding import PartitionSpec as P


REACH = 8
GRANT = 16 << 20


def make_band(order):
    rows = jnp.arange(order, dtype=jnp.int32)
    offset = (rows[:, None] - rows[None, :]).astype(jnp.float32)
    weights = jnp.exp(-(offset * offset) / (4.0 * REACH))
    inside = jnp.abs(offset) <= REACH
    return jnp.where(inside, weights, jnp.float32(0.0)).astype(jnp.bfloat16)


def by_rows(perturbations, gradient):
    local_rows, _, levels, columns = gradient.shape
    count_here = perturbations.shape[0]
    grid_rows = perturbations.shape[1]
    members = count_here * lax.axis_size("mem")
    band_x = make_band(columns)
    band_y = make_band(grid_rows)
    row_block = lax.all_to_all(perturbations, "mem", split_axis=1, concat_axis=0, tiled=True)
    mixed = jnp.sum(
        row_block.astype(jnp.float32) * gradient.astype(jnp.float32)[None], axis=2
    ).astype(jnp.bfloat16)
    along_x = jnp.dot(
        mixed.reshape(members * local_rows * levels, columns),
        band_x,
        preferred_element_type=jnp.float32,
    )
    along_x = along_x.astype(jnp.bfloat16).reshape(members, local_rows, levels, columns)
    whole_field = lax.all_to_all(along_x, "mem", split_axis=0, concat_axis=1, tiled=True)
    whole_field = whole_field.reshape(count_here, grid_rows, levels * columns)
    filtered = jnp.stack(
        [jnp.dot(band_y, field, preferred_element_type=jnp.float32) for field in whole_field]
    )
    filtered = filtered.astype(jnp.bfloat16).reshape(count_here, grid_rows, levels, columns)
    row_field = lax.all_to_all(filtered, "mem", split_axis=1, concat_axis=0, tiled=True)
    total = jnp.sum(
        row_block.astype(jnp.float32) * row_field.astype(jnp.float32)[:, :, None], axis=0
    )
    return (total * (1.0 / (members - 1))).astype(jnp.bfloat16)


HALF, PAIR, SIDE, CORE = 8, 4, 2, 1
PEERS = (PAIR + SIDE, SIDE, PAIR)


def swap(array, bits):
    return lax.ppermute(array, "mem", [(i, i ^ bits) for i in range(16)])


def edges(array):
    pairs = []
    for i in range(16):
        half, place, core = i // 8, i // 2 % 4, i % 2
        place = (place + (1 if core else 3)) % 4
        pairs.append((i, half * 8 + place * 2 + core))
    return lax.ppermute(array, "mem", pairs)


def first_row(strip, chip, rows):
    start = jnp.clip(chip * strip - REACH, 0, rows - strip - 2 * REACH)
    return start, chip * strip - start


def window_kernel(strip, wanted, member_ref, grad_ref, *refs):
    outs, sem = refs[:-1], refs[-1]
    me = lax.axis_index("mem")
    rows = member_ref.shape[0]
    copies = [pltpu.make_async_copy(grad_ref, outs[len(wanted)], sem.at[len(wanted)])]
    for k, bits in enumerate(wanted):
        start, _ = first_row(strip, (me ^ bits) // 2, rows)
        copies.append(pltpu.make_async_copy(member_ref.at[pl.ds(start, strip + 2 * REACH)], outs[k], sem.at[k]))
    for copy in copies:
        copy.start()
    for copy in copies:
        copy.wait()


def windows(member, grad, strip, wanted):
    shape = (strip + 2 * REACH,) + member.shape[1:]
    outs = [jax.ShapeDtypeStruct(shape, member.dtype)] * len(wanted) + [jax.ShapeDtypeStruct(grad.shape, grad.dtype)]
    return pl.pallas_call(
        functools.partial(window_kernel, strip, wanted),
        out_shape=outs,
        in_specs=[pl.BlockSpec(memory_space=pltpu.HBM)] * 2,
        out_specs=[pl.BlockSpec(memory_space=pltpu.VMEM)] * len(outs),
        scratch_shapes=[pltpu.SemaphoreType.DMA((len(outs),))],
        compiler_params=pltpu.CompilerParams(vmem_limit_bytes=GRANT),
        name="windows",
    )(member, grad)


def strip_kernel(rows, far, me_ref, a_ref, b_ref, c_ref, d_ref, block_ref, edge_ref, mate_ref, band_ref,
                 own_ref, other_ref, grad_ref, mixed_ref, total_ref):
    me = me_ref[0]
    core, place = me % 2, me // 2 % 4
    part, reach = block_ref.shape[0], edge_ref.shape[1]
    strip = 2 * part
    chips = rows // strip
    chip = (me ^ (HALF * far)) // 2
    _, at = first_row(strip, chip, rows)
    span = strip + 2 * reach

    grad_ref[...] = jnp.zeros_like(grad_ref)
    grad_ref[pl.ds(at + core * part, part)] = block_ref[...]
    grad_ref[pl.ds(at + (1 - core) * part, part)] = mate_ref[pl.ds(far * part, part)]
    before = jnp.where(place == 0, 1 - far, far)
    after = jnp.where(place == 3, 1 - far, far)

    @pl.when(jnp.logical_and(chip > 0, core == 0))
    def _():
        grad_ref[pl.ds(at - reach, reach)] = mate_ref[pl.ds(2 * part + before * reach, reach)]

    @pl.when(jnp.logical_and(chip > 0, core == 1))
    def _():
        grad_ref[pl.ds(at - reach, reach)] = edge_ref[before]

    @pl.when(jnp.logical_and(chip < chips - 1, core == 0))
    def _():
        grad_ref[pl.ds(at + strip, reach)] = edge_ref[after]

    @pl.when(jnp.logical_and(chip < chips - 1, core == 1))
    def _():
        grad_ref[pl.ds(at + strip, reach)] = mate_ref[pl.ds(2 * part + after * reach, reach)]

    grad = grad_ref[...].astype(jnp.float32)
    members = (a_ref, b_ref, c_ref, d_ref)
    nvars, columns = grad.shape[1:]
    grad = grad.reshape(span * nvars, columns)
    row = lax.broadcasted_iota(jnp.int32, (span, span * nvars), 1) // nvars
    pick = jnp.where(row == lax.broadcasted_iota(jnp.int32, row.shape, 0), 1.0, 0.0).astype(jnp.bfloat16)
    for k, ref in enumerate(members):
        terms = ref[...].reshape(span * nvars, columns).astype(jnp.float32) * grad
        high = terms.astype(jnp.bfloat16)
        low = (terms - high.astype(jnp.float32)).astype(jnp.bfloat16)
        mixed = jnp.dot(pick, high, preferred_element_type=jnp.float32)
        mixed = mixed + jnp.dot(pick, low, preferred_element_type=jnp.float32)
        mixed_ref[pl.ds(k * span, span)] = mixed.astype(jnp.bfloat16)
    along = jnp.dot(mixed_ref[...], band_ref[...], preferred_element_type=jnp.float32).astype(jnp.bfloat16)
    offset = lax.broadcasted_iota(jnp.int32, (strip, span), 0) + at - lax.broadcasted_iota(jnp.int32, (strip, span), 1)
    wide = offset.astype(jnp.float32)
    band = jnp.exp(-(wide * wide) / (4.0 * REACH))
    band = jnp.where(jnp.abs(wide) <= REACH, band, 0.0).astype(jnp.bfloat16)
    total = None
    for k, ref in enumerate(members):
        field = jnp.dot(band, along[k * span : (k + 1) * span], preferred_element_type=jnp.float32)
        field = field.astype(jnp.bfloat16).astype(jnp.float32)
        term = ref[pl.ds(at, strip)].astype(jnp.float32) * field[:, None, :]
        total = term if total is None else total + term
    total_ref[...] = total
    own_ref[...] = total_ref[pl.ds(core * part, part)].astype(own_ref.dtype)
    other_ref[...] = total_ref[pl.ds((1 - core) * part, part)].astype(other_ref.dtype)


def one_strip(me, members, block, edge, mate, band, rows, far):
    nvars, columns = block.shape[1:]
    part = block.shape[0]
    span = 2 * part + 2 * edge.shape[1]
    piece = (part, nvars, columns)
    vmem = pl.BlockSpec(memory_space=pltpu.VMEM)
    return pl.pallas_call(
        functools.partial(strip_kernel, rows, far),
        out_shape=[
            jax.ShapeDtypeStruct(piece, jnp.float32),
            jax.ShapeDtypeStruct(piece, jnp.bfloat16),
        ],
        in_specs=[pl.BlockSpec(memory_space=pltpu.SMEM)] + [vmem] * 8,
        out_specs=[vmem] * 2,
        scratch_shapes=[
            pltpu.VMEM((span, nvars, columns), jnp.bfloat16),
            pltpu.VMEM((4 * span, columns), jnp.bfloat16),
            pltpu.VMEM((2 * part, nvars, columns), jnp.float32),
        ],
        compiler_params=pltpu.CompilerParams(vmem_limit_bytes=GRANT),
        name="far" if far else "near",
    )(me, *members, block, edge, mate, band)


def by_halves(perturbations, gradient):
    local_rows, nvars, _, columns = gradient.shape
    grid_rows = perturbations.shape[1]
    strip = 2 * local_rows
    members = lax.axis_size("mem")
    at = lax.axis_index("mem")
    me = at.reshape(1).astype(jnp.int32)
    param = gradient.reshape(local_rows, nvars, columns)
    member = pltpu.with_memory_space_constraint(perturbations.reshape(-1, nvars, columns), pltpu.HBM)
    stays = pltpu.with_memory_space_constraint(param, pltpu.HBM)

    wanted = [p ^ HALF for p in PEERS] + list(PEERS) + [HALF, 0]
    there = swap(param, HALF)
    *out, far_mine, near_mine, here = windows(member, stays, strip, wanted)
    far_in = [far_mine] + [swap(block, p) for block, p in zip(out[:3], PEERS)]
    near_in = [near_mine] + [swap(block, p) for block, p in zip(out[3:], PEERS)]
    both = jnp.stack([here, there])
    both = jnp.where(at & 1 == 0, both[:, :REACH], both[:, -REACH:])
    edge = edges(both)
    early = swap(jnp.concatenate([here, there]), CORE)
    mate = jnp.concatenate([early, swap(jnp.concatenate([edge[0], edge[1]]), CORE)])

    band = make_band(columns)
    args = (edge, mate, band, grid_rows)
    far_own, far_other = one_strip(me, far_in, there, *args, 1)
    far_sum = far_own + swap(far_other, CORE).astype(jnp.float32)
    far_sum = swap(far_sum.astype(jnp.bfloat16), HALF).astype(jnp.float32)
    near_own, near_other = one_strip(me, near_in, here, *args, 0)
    near_other = swap(near_other, CORE)
    total = near_own + near_other.astype(jnp.float32) + far_sum
    return (total * (1.0 / (members - 1))).astype(jnp.bfloat16).reshape(gradient.shape)


def solution(mesh):
    in_specs = (P(("group", "mem"), None, None, None, None), P(("group", "mem"), None, None, None))
    out_specs = P(("group", "mem"), None, None, None)
    halves = mesh.shape["mem"] == 16

    def per_device(perturbations, gradient):
        count_here, grid_rows, _, levels, _ = perturbations.shape
        local_rows = gradient.shape[0]
        if not halves:
            return by_rows(perturbations, gradient)
        assert count_here == 1 and levels == 1 and local_rows % 8 == 0 and grid_rows == 16 * local_rows
        return by_halves(perturbations, gradient)

    return jax.shard_map(
        per_device, mesh=mesh, in_specs=in_specs, out_specs=out_specs, check_vma=False
    )
```

```python
import functools

import jax
import jax.numpy as jnp
import numpy as np
from jax import lax
from jax.experimental import pallas as pl
from jax.experimental.pallas import tpu as pltpu
from jax.sharding import PartitionSpec as P


REACH = 8
GRANT = 16 << 20


def make_band(order):
    rows = jnp.arange(order, dtype=jnp.int32)
    offset = (rows[:, None] - rows[None, :]).astype(jnp.float32)
    weights = jnp.exp(-(offset * offset) / (4.0 * REACH))
    inside = jnp.abs(offset) <= REACH
    return jnp.where(inside, weights, jnp.float32(0.0)).astype(jnp.bfloat16)


def fixed_band(order):
    offset = np.arange(order)[:, None] - np.arange(order)[None, :]
    weights = np.exp(-(offset.astype(np.float32) ** 2) / np.float32(4.0 * REACH))
    return np.where(np.abs(offset) <= REACH, weights, np.float32(0.0)).astype(jnp.bfloat16)


def by_rows(perturbations, gradient):
    local_rows, _, levels, columns = gradient.shape
    count_here = perturbations.shape[0]
    grid_rows = perturbations.shape[1]
    members = count_here * lax.axis_size("mem")
    band_x = make_band(columns)
    band_y = make_band(grid_rows)
    row_block = lax.all_to_all(perturbations, "mem", split_axis=1, concat_axis=0, tiled=True)
    mixed = jnp.sum(
        row_block.astype(jnp.float32) * gradient.astype(jnp.float32)[None], axis=2
    ).astype(jnp.bfloat16)
    along_x = jnp.dot(
        mixed.reshape(members * local_rows * levels, columns),
        band_x,
        preferred_element_type=jnp.float32,
    )
    along_x = along_x.astype(jnp.bfloat16).reshape(members, local_rows, levels, columns)
    whole_field = lax.all_to_all(along_x, "mem", split_axis=0, concat_axis=1, tiled=True)
    whole_field = whole_field.reshape(count_here, grid_rows, levels * columns)
    filtered = jnp.stack(
        [jnp.dot(band_y, field, preferred_element_type=jnp.float32) for field in whole_field]
    )
    filtered = filtered.astype(jnp.bfloat16).reshape(count_here, grid_rows, levels, columns)
    row_field = lax.all_to_all(filtered, "mem", split_axis=1, concat_axis=0, tiled=True)
    total = jnp.sum(
        row_block.astype(jnp.float32) * row_field.astype(jnp.float32)[:, :, None], axis=0
    )
    return (total * (1.0 / (members - 1))).astype(jnp.bfloat16)


HALF, PAIR, SIDE, CORE = 8, 4, 2, 1
PEERS = (PAIR + SIDE, SIDE, PAIR)


def swap(array, bits):
    return lax.ppermute(array, "mem", [(i, i ^ bits) for i in range(16)])


def edges(array):
    pairs = []
    for i in range(16):
        half, place, core = i // 8, i // 2 % 4, i % 2
        place = (place + (1 if core else 3)) % 4
        pairs.append((i, half * 8 + place * 2 + core))
    return lax.ppermute(array, "mem", pairs)


def first_row(strip, chip, rows):
    start = jnp.clip(chip * strip - REACH, 0, rows - strip - 2 * REACH)
    return start, chip * strip - start


def window_kernel(strip, wanted, member_ref, grad_ref, *refs):
    outs, sem = refs[:-1], refs[-1]
    me = lax.axis_index("mem")
    rows = member_ref.shape[0]
    copies = [pltpu.make_async_copy(grad_ref, outs[len(wanted)], sem.at[len(wanted)])]
    for k, bits in enumerate(wanted):
        start, _ = first_row(strip, (me ^ bits) // 2, rows)
        copies.append(pltpu.make_async_copy(member_ref.at[pl.ds(start, strip + 2 * REACH)], outs[k], sem.at[k]))
    for copy in copies:
        copy.start()
    for copy in copies:
        copy.wait()


def windows(member, grad, strip, wanted):
    shape = (strip + 2 * REACH,) + member.shape[1:]
    outs = [jax.ShapeDtypeStruct(shape, member.dtype)] * len(wanted) + [jax.ShapeDtypeStruct(grad.shape, grad.dtype)]
    return pl.pallas_call(
        functools.partial(window_kernel, strip, wanted),
        out_shape=outs,
        in_specs=[pl.BlockSpec(memory_space=pltpu.HBM)] * 2,
        out_specs=[pl.BlockSpec(memory_space=pltpu.VMEM)] * len(outs),
        scratch_shapes=[pltpu.SemaphoreType.DMA((len(outs),))],
        compiler_params=pltpu.CompilerParams(vmem_limit_bytes=GRANT),
        name="windows",
    )(member, grad)


def strip_kernel(rows, far, me_ref, a_ref, b_ref, c_ref, d_ref, block_ref, edge_ref, mate_ref, band_ref,
                 own_ref, other_ref, grad_ref, mixed_ref, total_ref):
    me = me_ref[0]
    core, place = me % 2, me // 2 % 4
    part, reach = block_ref.shape[0], edge_ref.shape[1]
    strip = 2 * part
    chips = rows // strip
    chip = (me ^ (HALF * far)) // 2
    _, at = first_row(strip, chip, rows)
    span = strip + 2 * reach

    grad_ref[...] = jnp.zeros_like(grad_ref)
    grad_ref[pl.ds(at + core * part, part)] = block_ref[...]
    grad_ref[pl.ds(at + (1 - core) * part, part)] = mate_ref[pl.ds(far * part, part)]
    before = jnp.where(place == 0, 1 - far, far)
    after = jnp.where(place == 3, 1 - far, far)

    @pl.when(jnp.logical_and(chip > 0, core == 0))
    def _():
        grad_ref[pl.ds(at - reach, reach)] = mate_ref[pl.ds(2 * part + before * reach, reach)]

    @pl.when(jnp.logical_and(chip > 0, core == 1))
    def _():
        grad_ref[pl.ds(at - reach, reach)] = edge_ref[before]

    @pl.when(jnp.logical_and(chip < chips - 1, core == 0))
    def _():
        grad_ref[pl.ds(at + strip, reach)] = edge_ref[after]

    @pl.when(jnp.logical_and(chip < chips - 1, core == 1))
    def _():
        grad_ref[pl.ds(at + strip, reach)] = mate_ref[pl.ds(2 * part + after * reach, reach)]

    grad = grad_ref[...].astype(jnp.float32)
    members = (a_ref, b_ref, c_ref, d_ref)
    nvars, columns = grad.shape[1:]
    grad = grad.reshape(span * nvars, columns)
    row = lax.broadcasted_iota(jnp.int32, (span, span * nvars), 1) // nvars
    pick = jnp.where(row == lax.broadcasted_iota(jnp.int32, row.shape, 0), 1.0, 0.0).astype(jnp.bfloat16)
    for k, ref in enumerate(members):
        terms = ref[...].reshape(span * nvars, columns).astype(jnp.float32) * grad
        high = terms.astype(jnp.bfloat16)
        low = (terms - high.astype(jnp.float32)).astype(jnp.bfloat16)
        mixed = jnp.dot(pick, high, preferred_element_type=jnp.float32)
        mixed = mixed + jnp.dot(pick, low, preferred_element_type=jnp.float32)
        mixed_ref[pl.ds(k * span, span)] = mixed.astype(jnp.bfloat16)
    along = jnp.dot(mixed_ref[...], band_ref[...], preferred_element_type=jnp.float32).astype(jnp.bfloat16)
    offset = lax.broadcasted_iota(jnp.int32, (strip, span), 0) + at - lax.broadcasted_iota(jnp.int32, (strip, span), 1)
    wide = offset.astype(jnp.float32)
    band = jnp.exp(-(wide * wide) / (4.0 * REACH))
    band = jnp.where(jnp.abs(wide) <= REACH, band, 0.0).astype(jnp.bfloat16)
    total = None
    for k, ref in enumerate(members):
        field = jnp.dot(band, along[k * span : (k + 1) * span], preferred_element_type=jnp.float32)
        field = field.astype(jnp.bfloat16).astype(jnp.float32)
        term = ref[pl.ds(at, strip)].astype(jnp.float32) * field[:, None, :]
        total = term if total is None else total + term
    total_ref[...] = total
    own_ref[...] = total_ref[pl.ds(core * part, part)].astype(own_ref.dtype)
    other_ref[...] = total_ref[pl.ds((1 - core) * part, part)].astype(other_ref.dtype)


def one_strip(me, members, block, edge, mate, band, rows, far):
    nvars, columns = block.shape[1:]
    part = block.shape[0]
    span = 2 * part + 2 * edge.shape[1]
    piece = (part, nvars, columns)
    vmem = pl.BlockSpec(memory_space=pltpu.VMEM)
    return pl.pallas_call(
        functools.partial(strip_kernel, rows, far),
        out_shape=[
            jax.ShapeDtypeStruct(piece, jnp.float32),
            jax.ShapeDtypeStruct(piece, jnp.bfloat16),
        ],
        in_specs=[pl.BlockSpec(memory_space=pltpu.SMEM)] + [vmem] * 8,
        out_specs=[vmem] * 2,
        scratch_shapes=[
            pltpu.VMEM((span, nvars, columns), jnp.bfloat16),
            pltpu.VMEM((4 * span, columns), jnp.bfloat16),
            pltpu.VMEM((2 * part, nvars, columns), jnp.float32),
        ],
        compiler_params=pltpu.CompilerParams(vmem_limit_bytes=GRANT),
        name="far" if far else "near",
    )(me, *members, block, edge, mate, band)


def by_halves(perturbations, gradient):
    local_rows, nvars, _, columns = gradient.shape
    grid_rows = perturbations.shape[1]
    strip = 2 * local_rows
    members = lax.axis_size("mem")
    at = lax.axis_index("mem")
    me = at.reshape(1).astype(jnp.int32)
    param = gradient.reshape(local_rows, nvars, columns)
    member = pltpu.with_memory_space_constraint(perturbations.reshape(-1, nvars, columns), pltpu.HBM)
    stays = pltpu.with_memory_space_constraint(param, pltpu.HBM)

    wanted = [p ^ HALF for p in PEERS] + list(PEERS) + [HALF, 0]
    there = swap(param, HALF)
    *out, far_mine, near_mine, here = windows(member, stays, strip, wanted)
    far_in = [far_mine] + [swap(block, p) for block, p in zip(out[:3], PEERS)]
    near_in = [near_mine] + [swap(block, p) for block, p in zip(out[3:], PEERS)]
    both = jnp.stack([here, there])
    both = jnp.where(at & 1 == 0, both[:, :REACH], both[:, -REACH:])
    edge = edges(both)
    early = swap(jnp.concatenate([here, there]), CORE)
    mate = jnp.concatenate([early, swap(jnp.concatenate([edge[0], edge[1]]), CORE)])

    band = jnp.asarray(fixed_band(columns))
    args = (edge, mate, band, grid_rows)
    far_own, far_other = one_strip(me, far_in, there, *args, 1)
    far_sum = far_own + swap(far_other, CORE).astype(jnp.float32)
    far_sum = swap(far_sum.astype(jnp.bfloat16), HALF).astype(jnp.float32)
    near_own, near_other = one_strip(me, near_in, here, *args, 0)
    near_other = swap(near_other, CORE)
    total = near_own + near_other.astype(jnp.float32) + far_sum
    return (total * (1.0 / (members - 1))).astype(jnp.bfloat16).reshape(gradient.shape)


def solution(mesh):
    in_specs = (P(("group", "mem"), None, None, None, None), P(("group", "mem"), None, None, None))
    out_specs = P(("group", "mem"), None, None, None)
    halves = mesh.shape["mem"] == 16

    def per_device(perturbations, gradient):
        count_here, grid_rows, _, levels, _ = perturbations.shape
        local_rows = gradient.shape[0]
        if not halves:
            return by_rows(perturbations, gradient)
        assert count_here == 1 and levels == 1 and local_rows % 8 == 0 and grid_rows == 16 * local_rows
        return by_halves(perturbations, gradient)

    return jax.shard_map(
        per_device, mesh=mesh, in_specs=in_specs, out_specs=out_specs, check_vma=False
    )
```
